1024 devices in a mesh: layer: 256 (over y, z_hi, x), dp: 4 (over z_lo, core).
Axes of the slice: x: 8, y: 8, z: 8 (z_hi: 4, z_lo: 2; z = z_hi * 2 + z_lo), core: 2. Of those that a mesh axis runs over, the one named last changes fastest.
Arguments:
- activations: bfloat16 [256, 512, 8192], P('layer', 'dp'), may hold values from -6 to 6
- gradients: bfloat16 [256, 512, 896], P('layer', 'dp'), may hold values from -6 to 6
- input_factor: bfloat16 [256, 8192, 256], P('layer', 'dp'), may hold values from -0.0625 to 0.0625
- output_factor: bfloat16 [256, 896, 256], P('layer', 'dp'), may hold values from -0.1875 to 0.1875
- lengths: int32 [16], P('dp'), may hold values from 1 to 32, 320 in all
Outputs:
- influence: float32 [16, 8], P('dp')
The draws below stay inside these ranges and needn't reach their ends.
Inputs may be any that keep to these rules, and one draw needn't show every extreme that they name: `lengths`: each sequence's live tokens fill the front of its slots; the counts sum to 320 and one sequence fills all 32 slots.
All inputs are finite; a program needn't handle non-finite values. No bound on the sum of `lengths` on one device may be relied on, other than what follows from the above.
Results may differ from the reference program's by a relative error of at most 0.0003.
Values may be sent and summed in bfloat16 or wider, within the bound.
A program may use at most 32 MiB of HBM per device.

```python
import math
import jax
import jax.numpy as jnp
import numpy as np
from jax import lax

D = 8192
RANK = 32
QUERIES = 8
SLOT = 32
TILE = 896
BLOCKS = 256
SEQS = 16
TOKENS = 512


def block_levels(own_key, dims, cuts, smallest, high):
    def one(dim, shards_of):
        draws = jax.random.uniform(jax.random.fold_in(jax.random.fold_in(own_key, 6), dim), (shards_of,), jnp.float32, smallest / len(cuts), high / len(cuts))
        return jnp.repeat(jnp.exp(draws), dims[dim] // shards_of).reshape((-1,) + (1,) * (len(dims) - dim - 1))

    level = one(*cuts[0])
    for cut in cuts[1:]:
        level = level * one(*cut)
    return level


def length_profile(number_of, total, most, skew):
    loads = [(1 << 20) // math.isqrt(grade ** skew) + 1 for grade in range(2, number_of + 1)]
    surplus, given = total - most - (number_of - 1), [1] * (number_of - 1)
    while surplus > 0:
        candidates = [i for i in range(number_of - 1) if given[i] < most]
        pool, remaining = sum([loads[i] for i in candidates]), surplus
        for i in candidates:
            extra = min(most - given[i], max(1, remaining * loads[i] // pool), surplus)
            given[i] = given[i] + extra
            surplus = surplus - extra
    return np.array([most] + given)


def ragged_sizes(key, amount, total, most, slope):
    if amount == 2:
        one = jax.random.randint(key, (), max(1, total - most), min(most, total - 1) + 1)
        return jnp.stack([one, total - one])
    sizes = jnp.asarray(length_profile(amount, total, most, slope), jnp.int32)
    twos = (amount - 1) // 2
    donor, sink = sizes[1:1 + 2 * twos:2], sizes[2:2 + 2 * twos:2]
    slack = jnp.minimum(donor - 1, most - sink)
    shifted = jax.random.randint(jax.random.fold_in(key, 1), (twos,), 0, 1 << 20) % (slack + 1)
    sizes = sizes.at[1:1 + 2 * twos:2].set(donor - shifted).at[2:2 + 2 * twos:2].set(sink + shifted)
    return sizes[jax.random.permutation(jax.random.fold_in(key, 2), amount)]


def noise(key, shape, deviation, most, split=(), held_as=jnp.bfloat16):
    factor_of = block_levels(key, shape, split, -0.22, 0.18) if split else 1.0
    entries = jax.random.normal(key, shape, jnp.float32) * deviation * factor_of
    return jnp.minimum(jnp.maximum(entries, -most), most).astype(held_as)


def setup_inputs(seed: int = 0) -> dict:
    streams_of = jax.random.split(jax.random.key(seed), 6)
    activations = noise(streams_of[0], (BLOCKS, TOKENS, D), 1.0, 6.0, ((0, 256), (1, 4)))
    gradients = noise(streams_of[1], (BLOCKS, TOKENS, TILE), 1.0, 6.0, ((0, 256), (1, 4)))
    input_factor = noise(streams_of[2], (BLOCKS, D, QUERIES * RANK), D ** -0.5, 0.0625, ((0, 256), (1, 4)))
    output_factor = noise(streams_of[3], (BLOCKS, TILE, QUERIES * RANK), TILE ** -0.5, 0.1875, ((0, 256), (1, 4)))
    lengths = ragged_sizes(streams_of[4], SEQS, 5 * SEQS * SLOT // 8, SLOT, 0).astype(jnp.int32)
    return {"activations": activations, "gradients": gradients, "input_factor": input_factor, "output_factor": output_factor, "lengths": lengths}


def live_tokens(lengths, count):
    position = jnp.arange(count, dtype=jnp.int32)
    sequence = position // SLOT
    owners = sequence[:, None] == jnp.arange(lengths.shape[0], dtype=jnp.int32)[None, :]
    limit = lax.optimization_barrier(jnp.sum(jnp.where(owners, lengths[None, :], 0), axis=1))
    return (position % SLOT < limit).astype(jnp.float32)

def block_scores(block):
    inputs, grads, in_factor, out_factor = block
    projected_in = jnp.dot(inputs, in_factor, preferred_element_type=jnp.float32)
    projected_out = jnp.dot(grads, out_factor, preferred_element_type=jnp.float32)
    return lax.optimization_barrier(jnp.sum((projected_in * projected_out).reshape(TOKENS, QUERIES, RANK), axis=2))

def reference(activations, gradients, input_factor, output_factor, lengths):
    scores = lax.map(block_scores, (activations, gradients, input_factor, output_factor))
    total = lax.optimization_barrier(jnp.sum(scores, axis=0))
    live = live_tokens(lengths, TOKENS)
    per_sequence = lax.optimization_barrier(jnp.sum((total * live[:, None]).reshape(SEQS, SLOT, QUERIES), axis=1))
    return per_sequence / jnp.float32(math.sqrt(RANK * SLOT * BLOCKS))
```

```python
import functools
import math

import jax
import jax.numpy as jnp
from jax import lax
from jax.experimental import pallas as pl
from jax.experimental.pallas import tpu as pltpu
from jax.sharding import PartitionSpec as P

RANK = 32
QUERIES = 8
SLOT = 32
LANES = 128
MESH = pl.DeviceIdType.MESH
LAYER_DIMS = {256: (8, 4, 8), 8: (2, 2, 2), 4: (2, 1, 2)}
CHUNKS = 8


def kernel(
    dims, blocks, act, grad, inf, outf, lens, out,
    act_v, grad_v, of_v, if_v, len_v, pi, po, rx1, rx2, rx3,
    local_sem, out_send, out_recv, core_send, core_recv, if_send, if_recv,
    send1, recv1, send2, recv2, send3, recv3,
):
    ny, nz, nx = dims
    layer, dp = lax.axis_index("layer"), lax.axis_index("dp")
    x = lax.rem(layer, nx)
    z = lax.rem(layer // nx, nz)
    y = layer // (nx * nz)
    core = lax.rem(dp, 2)
    chip = dp // 2
    partner = chip * 2 + 1 - core
    cross = (1 - chip) * 2 + core
    tokens, depth = act.shape[1], inf.shape[1]
    odepth = outf.shape[1]
    step = depth // CHUNKS

    def at(y_, z_, x_):
        return (y_ * nz + z_) * nx + x_

    first = [(d, o) for o in (0, 1) for d in range(nx) if d or o]

    def peer1(d, o):
        c = core if o == 0 else 1 - core
        return {"layer": at(y, z, lax.rem(x + d, nx)), "dp": chip * 2 + c}

    def peer2(d):
        return {"layer": at(lax.rem(y + d, ny), z, x), "dp": dp}

    def peer3(d):
        return {"layer": at(y, lax.rem(z + d, nz), x), "dp": dp}

    barrier = pltpu.get_barrier_semaphore()
    peers = [{"layer": layer, "dp": cross}]
    peers += [peer1(d, o) for d, o in first]
    peers += [peer2(d) for d in range(1, ny)]
    peers += [peer3(d) for d in range(1, nz)]
    for peer in peers:
        pl.semaphore_signal(barrier, inc=1, device_id=peer, device_id_type=MESH)

    def columns(shard):
        return pl.ds(pl.multiple_of(shard * depth, LANES), depth)

    mine = pl.ds(pl.multiple_of(core * tokens, 128), tokens)
    local = [
        pltpu.make_async_copy(act.at[0, :, columns(dp)], act_v.at[0, mine, :], local_sem.at[0]),
        pltpu.make_async_copy(act.at[0, :, columns(cross)], act_v.at[1, mine, :], local_sem.at[1]),
        pltpu.make_async_copy(grad.at[0], grad_v.at[mine, :], local_sem.at[2]),
        pltpu.make_async_copy(inf.at[0], if_v.at[0], local_sem.at[3]),
        pltpu.make_async_copy(outf.at[0], of_v.at[dp], local_sem.at[4]),
        pltpu.make_async_copy(lens, len_v.at[core], local_sem.at[5]),
    ]
    for copy in local:
        copy.start()
    pl.semaphore_wait(barrier, len(peers))

    def remote(src, dst, send, recv, device):
        return pltpu.make_async_remote_copy(
            src_ref=src, dst_ref=dst, send_sem=send, recv_sem=recv, device_id=device, device_id_type=MESH
        )

    over = {"layer": layer, "dp": cross}
    beside = {"layer": layer, "dp": partner}
    out_over = remote(outf.at[0], of_v.at[dp], out_send, out_recv, over)
    out_over.start()

    def chunk(i):
        rows = pl.ds(pl.multiple_of(i * step, 16), step)
        return remote(inf.at[0, rows, :], if_v.at[1, rows, :], if_send.at[i], if_recv.at[i], over)

    for i in range(CHUNKS):
        chunk(i).start()

    partner_cross = (1 - chip) * 2 + 1 - core
    swaps = [
        remote(lens, len_v.at[core], core_send.at[0], core_recv.at[0], beside),
        remote(outf.at[0], of_v.at[dp], core_send.at[1], core_recv.at[1], beside),
        remote(grad.at[0], grad_v.at[mine, :], core_send.at[2], core_recv.at[2], beside),
        remote(act.at[0, :, columns(partner)], act_v.at[0, mine, :], core_send.at[3], core_recv.at[3], beside),
        remote(act.at[0, :, columns(partner_cross)], act_v.at[1, mine, :], core_send.at[4], core_recv.at[4], beside),
    ]
    for copy in swaps:
        copy.start()
    relay = remote(of_v.at[cross], of_v.at[cross], core_send.at[5], core_recv.at[5], beside)

    for copy in local:
        copy.wait()
    for copy in swaps:
        copy.wait()

    def contract(block):
        def body(i, carry):
            rows = pl.ds(pl.multiple_of(i * step, LANES), step)
            if block == 1:
                chunk(i).wait()
            product = jnp.dot(act_v[block, :, rows], if_v[block, rows, :], preferred_element_type=jnp.float32)
            if block == 0:
                pi[...] = jnp.where(i == 0, product, pi[...] + product)
            else:
                pi[...] += product
            return carry

        lax.fori_loop(0, CHUNKS, body, 0)

    out_over.wait()
    relay.start()
    pi[...] = jnp.zeros_like(pi)
    contract(0)
    relay.wait()

    seqs = tokens // SLOT
    row = lax.broadcasted_iota(jnp.int32, (2 * tokens, 1), 0)
    limit = jnp.zeros((2 * tokens, 1), jnp.int32)
    for s in range(2 * seqs):
        count = len_v[s // seqs][:, s % seqs : s % seqs + 1]
        limit = jnp.where(row // SLOT == s, count, limit)
    live = (row % SLOT < limit).astype(jnp.float32)
    total = jnp.zeros(po.shape, jnp.float32)
    for shard in range(4):
        total += jnp.dot(
            grad_v[:, shard * odepth : (shard + 1) * odepth], of_v[shard], preferred_element_type=jnp.float32
        )
    po[...] = total * live
    contract(1)

    width = QUERIES * RANK
    lanes = lax.broadcasted_iota(jnp.int32, (width, LANES), 1)
    fold = (lax.broadcasted_iota(jnp.int32, (width, LANES), 0) // RANK == lanes % QUERIES).astype(jnp.float32)
    score = jnp.sum((po[...] * pi[...]).reshape(2 * seqs, SLOT, width), axis=1)
    score = jnp.dot(score, fold, precision=lax.Precision.HIGHEST, preferred_element_type=jnp.float32)
    spot = lax.broadcasted_iota(jnp.int32, (2 * seqs, LANES), 1) // QUERIES
    keep = spot == lax.broadcasted_iota(jnp.int32, (2 * seqs, LANES), 0)
    value = jnp.sum(jnp.where(keep, score, 0.0), axis=0, keepdims=True)

    def exchange(value, rx, me, sends):
        rx[me] = value
        copies = [remote(rx.at[me], rx.at[me], s, r, device) for s, r, device in sends]
        for copy in copies:
            copy.start()
        for copy in copies:
            copy.wait()
        result = rx[0]
        for j in range(1, rx.shape[0]):
            result = result + rx[j]
        return result

    value = exchange(
        value, rx1, core * nx + x, [(send1.at[i], recv1.at[i], peer1(d, o)) for i, (d, o) in enumerate(first)]
    )
    value = exchange(value, rx2, y, [(send2.at[d], recv2.at[d], peer2(d)) for d in range(1, ny)])
    if nz > 1:
        value = exchange(value, rx3, z, [(send3.at[d], recv3.at[d], peer3(d)) for d in range(1, nz)])

    own = lax.broadcasted_iota(jnp.int32, (8, LANES), 0) + core * seqs
    lane = lax.broadcasted_iota(jnp.int32, (8, LANES), 1)
    spread = jnp.where(lane // QUERIES == own, jnp.broadcast_to(value, (8, LANES)), 0.0)
    gather = (
        lax.broadcasted_iota(jnp.int32, (LANES, LANES), 0) % QUERIES
        == lax.broadcasted_iota(jnp.int32, (LANES, LANES), 1)
    ).astype(jnp.float32)
    final = jnp.dot(spread, gather, precision=lax.Precision.HIGHEST, preferred_element_type=jnp.float32)
    out[...] = final[:seqs, :QUERIES] / jnp.float32(math.sqrt(RANK * SLOT * blocks))


def shards(activations, gradients, input_factor, output_factor, lengths):
    blocks = lax.axis_size("layer")
    dims = LAYER_DIMS[blocks]
    ny, nz, nx = dims
    tokens = activations.shape[1]
    depth, width = input_factor.shape[1:]
    odepth = output_factor.shape[1]
    seqs = lengths.shape[0]
    bf16, f32 = jnp.bfloat16, jnp.float32
    dma = pltpu.SemaphoreType.DMA
    anywhere = pl.BlockSpec(memory_space=pl.ANY)
    return pl.pallas_call(
        functools.partial(kernel, dims, blocks),
        out_shape=jax.ShapeDtypeStruct((seqs, QUERIES), f32),
        in_specs=[anywhere] * 5,
        out_specs=pl.BlockSpec(memory_space=pltpu.VMEM),
        scratch_shapes=[
            pltpu.VMEM((2, 2 * tokens, depth), bf16),
            pltpu.VMEM((2 * tokens, 4 * odepth), bf16),
            pltpu.VMEM((4, odepth, width), bf16),
            pltpu.VMEM((2, depth, width), bf16),
            pltpu.VMEM((2, 1, seqs), jnp.int32),
            pltpu.VMEM((2 * tokens, width), f32),
            pltpu.VMEM((2 * tokens, width), f32),
            pltpu.VMEM((2 * nx, 1, LANES), f32),
            pltpu.VMEM((ny, 1, LANES), f32),
            pltpu.VMEM((nz, 1, LANES), f32),
            dma((6,)),
            dma, dma,
            dma((6,)), dma((6,)),
            dma((CHUNKS,)), dma((CHUNKS,)),
            dma((2 * nx,)), dma((2 * nx,)),
            dma((ny,)), dma((ny,)),
            dma((nz,)), dma((nz,)),
        ],
        compiler_params=pltpu.CompilerParams(collective_id=0, has_side_effects=True),
    )(activations, gradients, input_factor, output_factor, lengths.reshape(1, seqs))


def solution(mesh):
    in_specs = (
        P("layer", "dp", None),
        P("layer", "dp", None),
        P("layer", "dp", None),
        P("layer", "dp", None),
        P("dp"),
    )
    out_specs = P("dp", None)
    return jax.shard_map(shards, mesh=mesh, in_specs=in_specs, out_specs=out_specs, check_vma=False)
```

```python
import functools
import math

import jax
import jax.numpy as jnp
from jax import lax
from jax.experimental import pallas as pl
from jax.experimental.pallas import tpu as pltpu
from jax.sharding import PartitionSpec as P

RANK = 32
QUERIES = 8
SLOT = 32
LANES = 128
MESH = pl.DeviceIdType.MESH
LAYER_DIMS = {256: (8, 4, 8), 8: (2, 2, 2), 4: (2, 1, 2)}
CHUNKS = 8
ROUNDS = 3


def kernel(
    dims, blocks, act, grad, inf, outf, lens, out,
    act_v, grad_v, of_v, if_v, len_v, pi, po, rx1, rx2, rx3,
    local_sem, out_send, out_recv, core_send, core_recv, if_send, if_recv,
    rounds, send1, recv1, send2, recv2, send3, recv3,
):
    ny, nz, nx = dims
    layer, dp = lax.axis_index("layer"), lax.axis_index("dp")
    x = lax.rem(layer, nx)
    z = lax.rem(layer // nx, nz)
    y = layer // (nx * nz)
    core = lax.rem(dp, 2)
    chip = dp // 2
    partner = chip * 2 + 1 - core
    cross = (1 - chip) * 2 + core
    tokens, depth = act.shape[1], inf.shape[1]
    odepth = outf.shape[1]
    step = depth // CHUNKS

    def at(y_, z_, x_):
        return (y_ * nz + z_) * nx + x_

    def far_first(n):
        return sorted(range(1, n), key=lambda d: -min(d, n - d))

    first = [(d, o) for d in far_first(nx) for o in (0, 1)] + [(0, 1)]

    def peer1(d, o):
        c = core if o == 0 else 1 - core
        return {"layer": at(y, z, lax.rem(x + d, nx)), "dp": chip * 2 + c}

    def peer2(d):
        return {"layer": at(lax.rem(y + d, ny), z, x), "dp": dp}

    def peer3(d):
        return {"layer": at(y, lax.rem(z + d, nz), x), "dp": dp}

    def remote(src, dst, send, recv, device):
        return pltpu.make_async_remote_copy(
            src_ref=src, dst_ref=dst, send_sem=send, recv_sem=recv, device_id=device, device_id_type=MESH
        )

    over = {"layer": layer, "dp": cross}
    beside = {"layer": layer, "dp": partner}

    barrier = pltpu.get_barrier_semaphore()
    next_z = {"layer": at(y, lax.rem(z + 2 * chip + nz - 1, nz), x), "dp": cross}
    near = [over, next_z, peer1(1, 0), peer1(nx - 1, 0), peer2(1), peer2(ny - 1)]
    for peer in [*near, beside]:
        pl.semaphore_signal(barrier, inc=1, device_id=peer, device_id_type=MESH)
    pl.semaphore_wait(barrier, len(near) + 1)

    out_over = remote(outf.at[0], of_v.at[dp], out_send, out_recv, over)
    out_over.start()

    def chunk(i):
        rows = pl.ds(pl.multiple_of(i * step, 16), step)
        return remote(inf.at[0, rows, :], if_v.at[1, rows, :], if_send.at[i], if_recv.at[i], over)

    for i in range(CHUNKS):
        chunk(i).start()

    def columns(shard):
        return pl.ds(pl.multiple_of(shard * depth, LANES), depth)

    mine = pl.ds(pl.multiple_of(core * tokens, 128), tokens)
    partner_cross = (1 - chip) * 2 + 1 - core
    swaps = [
        remote(lens, len_v.at[core], core_send.at[0], core_recv.at[0], beside),
        remote(outf.at[0], of_v.at[dp], core_send.at[1], core_recv.at[1], beside),
        remote(grad.at[0], grad_v.at[mine, :], core_send.at[2], core_recv.at[2], beside),
        remote(act.at[0, :, columns(partner)], act_v.at[0, mine, :], core_send.at[3], core_recv.at[3], beside),
        remote(act.at[0, :, columns(partner_cross)], act_v.at[1, mine, :], core_send.at[4], core_recv.at[4], beside),
    ]
    for copy in swaps:
        copy.start()
    local = [
        pltpu.make_async_copy(act.at[0, :, columns(dp)], act_v.at[0, mine, :], local_sem.at[0]),
        pltpu.make_async_copy(act.at[0, :, columns(cross)], act_v.at[1, mine, :], local_sem.at[1]),
        pltpu.make_async_copy(grad.at[0], grad_v.at[mine, :], local_sem.at[2]),
        pltpu.make_async_copy(inf.at[0], if_v.at[0], local_sem.at[3]),
        pltpu.make_async_copy(outf.at[0], of_v.at[dp], local_sem.at[4]),
        pltpu.make_async_copy(lens, len_v.at[core], local_sem.at[5]),
    ]
    for copy in local:
        copy.start()
    for r in range(ROUNDS):
        for peer in near:
            pl.semaphore_signal(rounds.at[r], inc=1, device_id=peer, device_id_type=MESH)
        pl.semaphore_wait(rounds.at[r], len(near))
    pl.semaphore_signal(rounds.at[ROUNDS], inc=1, device_id=beside, device_id_type=MESH)
    pl.semaphore_wait(rounds.at[ROUNDS], 1)

    relay = remote(of_v.at[cross], of_v.at[cross], core_send.at[5], core_recv.at[5], beside)

    for copy in local:
        copy.wait()
    for copy in swaps:
        copy.wait()

    def contract(block):
        def body(i, carry):
            rows = pl.ds(pl.multiple_of(i * step, LANES), step)
            if block == 1:
                chunk(i).wait_recv()
            product = jnp.dot(act_v[block, :, rows], if_v[block, rows, :], preferred_element_type=jnp.float32)
            if block == 0:
                pi[...] = jnp.where(i == 0, product, pi[...] + product)
            else:
                pi[...] += product
            return carry

        lax.fori_loop(0, CHUNKS, body, 0)

    out_over.wait()
    relay.start()
    pi[...] = jnp.zeros_like(pi)
    contract(0)
    relay.wait()

    seqs = tokens // SLOT
    row = lax.broadcasted_iota(jnp.int32, (2 * tokens, 1), 0)
    limit = jnp.zeros((2 * tokens, 1), jnp.int32)
    for s in range(2 * seqs):
        count = len_v[s // seqs][:, s % seqs : s % seqs + 1]
        limit = jnp.where(row // SLOT == s, count, limit)
    live = (row % SLOT < limit).astype(jnp.float32)
    total = jnp.zeros(po.shape, jnp.float32)
    for shard in range(4):
        total += jnp.dot(
            grad_v[:, shard * odepth : (shard + 1) * odepth], of_v[shard], preferred_element_type=jnp.float32
        )
    po[...] = total * live
    contract(1)

    width = QUERIES * RANK
    lanes = lax.broadcasted_iota(jnp.int32, (width, LANES), 1)
    fold = (lax.broadcasted_iota(jnp.int32, (width, LANES), 0) // RANK == lanes % QUERIES).astype(jnp.bfloat16)
    score = jnp.sum((po[...] * pi[...]).reshape(2 * seqs, SLOT, width), axis=1)
    high = score.astype(jnp.bfloat16).astype(jnp.float32)
    middle = (score - high).astype(jnp.bfloat16).astype(jnp.float32)
    parts = jnp.concatenate([high, middle, score - high - middle], axis=0).astype(jnp.bfloat16)
    score = jnp.sum(
        jnp.dot(parts, fold, preferred_element_type=jnp.float32).reshape(3, 2 * seqs, LANES), axis=0
    )
    spot = lax.broadcasted_iota(jnp.int32, (2 * seqs, LANES), 1) // QUERIES
    keep = spot == lax.broadcasted_iota(jnp.int32, (2 * seqs, LANES), 0)
    value = jnp.sum(jnp.where(keep, score, 0.0), axis=0, keepdims=True)

    waiting = [chunk(i) for i in range(CHUNKS)]

    def exchange(value, rx, me, sends):
        rx[me] = value
        copies = [remote(rx.at[me], rx.at[me], s, r, device) for s, r, device in sends]
        for copy in copies:
            copy.start()
        for copy in copies:
            copy.wait_recv()
        waiting.extend(copies)
        result = rx[0]
        for j in range(1, rx.shape[0]):
            result = result + rx[j]
        return result

    value = exchange(
        value, rx1, core * nx + x, [(send1.at[i], recv1.at[i], peer1(d, o)) for i, (d, o) in enumerate(first)]
    )
    value = exchange(value, rx2, y, [(send2.at[d], recv2.at[d], peer2(d)) for d in range(1, ny)])
    if nz > 1:
        value = exchange(value, rx3, z, [(send3.at[d], recv3.at[d], peer3(d)) for d in range(1, nz)])

    own = lax.broadcasted_iota(jnp.int32, (8, LANES), 0) + core * seqs
    lane = lax.broadcasted_iota(jnp.int32, (8, LANES), 1)
    spread = jnp.where(lane // QUERIES == own, jnp.broadcast_to(value, (8, LANES)), 0.0)
    for shift in (8, 16, 32, 64):
        spread += pltpu.roll(spread, shift, 1)
    out[...] = spread[:seqs, :QUERIES] * jnp.float32(1 / math.sqrt(RANK * SLOT * blocks))
    for copy in waiting:
        copy.wait_send()


def shards(activations, gradients, input_factor, output_factor, lengths):
    blocks = lax.axis_size("layer")
    dims = LAYER_DIMS[blocks]
    ny, nz, nx = dims
    tokens = activations.shape[1]
    depth, width = input_factor.shape[1:]
    odepth = output_factor.shape[1]
    seqs = lengths.shape[0]
    bf16, f32 = jnp.bfloat16, jnp.float32
    dma = pltpu.SemaphoreType.DMA
    anywhere = pl.BlockSpec(memory_space=pl.ANY)
    return pl.pallas_call(
        functools.partial(kernel, dims, blocks),
        out_shape=jax.ShapeDtypeStruct((seqs, QUERIES), f32),
        in_specs=[anywhere] * 5,
        out_specs=pl.BlockSpec(memory_space=pltpu.VMEM),
        scratch_shapes=[
            pltpu.VMEM((2, 2 * tokens, depth), bf16),
            pltpu.VMEM((2 * tokens, 4 * odepth), bf16),
            pltpu.VMEM((4, odepth, width), bf16),
            pltpu.VMEM((2, depth, width), bf16),
            pltpu.VMEM((2, 1, seqs), jnp.int32),
            pltpu.VMEM((2 * tokens, width), f32),
            pltpu.VMEM((2 * tokens, width), f32),
            pltpu.VMEM((2 * nx, 1, LANES), f32),
            pltpu.VMEM((ny, 1, LANES), f32),
            pltpu.VMEM((nz, 1, LANES), f32),
            dma((6,)),
            dma, dma,
            dma((6,)), dma((6,)),
            dma((CHUNKS,)), dma((CHUNKS,)),
            pltpu.SemaphoreType.REGULAR((ROUNDS + 1,)),
            dma((2 * nx,)), dma((2 * nx,)),
            dma((ny,)), dma((ny,)),
            dma((nz,)), dma((nz,)),
        ],
        compiler_params=pltpu.CompilerParams(collective_id=0, has_side_effects=True, vmem_limit_bytes=56500000),
    )(activations, gradients, input_factor, output_factor, lengths.reshape(1, seqs))


def solution(mesh):
    in_specs = (
        P("layer", "dp", None),
        P("layer", "dp", None),
        P("layer", "dp", None),
        P("layer", "dp", None),
        P("dp"),
    )
    out_specs = P("dp", None)
    return jax.shard_map(shards, mesh=mesh, in_specs=in_specs, out_specs=out_specs, check_vma=False)
```

```python
import functools
import math

import jax
import jax.numpy as jnp
from jax import lax
from jax.experimental import pallas as pl
from jax.experimental.pallas import tpu as pltpu
from jax.sharding import PartitionSpec as P

RANK = 32
QUERIES = 8
SLOT = 32
LANES = 128
MESH = pl.DeviceIdType.MESH
LAYER_DIMS = {256: (8, 4, 8), 8: (2, 2, 2), 4: (2, 1, 2)}
CHUNKS = 8
ROUNDS = 7


def kernel(
    dims, blocks, act, grad, inf, outf, lens, out,
    act_v, grad_v, of_v, if_v, len_v, pi, po, rx1, rx2,
    local_sem, out_send, out_recv, core_send, core_recv, if_send, if_recv,
    rounds, send1, recv1, send2, recv2,
):
    ny, nz, nx = dims
    layer, dp = lax.axis_index("layer"), lax.axis_index("dp")
    x = lax.rem(layer, nx)
    z = lax.rem(layer // nx, nz)
    y = layer // (nx * nz)
    core = lax.rem(dp, 2)
    chip = dp // 2
    partner = chip * 2 + 1 - core
    cross = (1 - chip) * 2 + core
    tokens, depth = act.shape[1], inf.shape[1]
    odepth = outf.shape[1]
    step = depth // CHUNKS

    def at(y_, z_, x_):
        return (y_ * nz + z_) * nx + x_

    def far_first(n):
        return sorted(range(1, n), key=lambda d: -min(d, n - d))

    first = [(d, o) for d in far_first(nx) for o in (0, 1)] + [(0, 1)]

    def peer1(d, o):
        c = core if o == 0 else 1 - core
        return {"layer": at(y, z, lax.rem(x + d, nx)), "dp": chip * 2 + c}

    second = [(d, e) for d in range(ny) for e in range(nz) if d or e]
    second.sort(key=lambda t: -min(t[0], ny - t[0]) - 2 * min(t[1], nz - t[1]))

    def peer2(d, e):
        return {"layer": at(lax.rem(y + d, ny), lax.rem(z + e, nz), x), "dp": dp}

    def remote(src, dst, send, recv, device):
        return pltpu.make_async_remote_copy(
            src_ref=src, dst_ref=dst, send_sem=send, recv_sem=recv, device_id=device, device_id_type=MESH
        )

    over = {"layer": layer, "dp": cross}
    beside = {"layer": layer, "dp": partner}

    barrier = pltpu.get_barrier_semaphore()
    next_z = {"layer": at(y, lax.rem(z + 2 * chip + nz - 1, nz), x), "dp": cross}
    near = [over, next_z, peer1(1, 0), peer1(nx - 1, 0), peer2(1, 0), peer2(ny - 1, 0)]
    for peer in [*near, beside]:
        pl.semaphore_signal(barrier, inc=1, device_id=peer, device_id_type=MESH)
    pl.semaphore_wait(barrier, len(near) + 1)

    out_over = remote(outf.at[0], of_v.at[dp], out_send, out_recv, over)
    out_over.start()

    def chunk(i):
        rows = pl.ds(pl.multiple_of(i * step, 16), step)
        return remote(inf.at[0, rows, :], if_v.at[1, rows, :], if_send.at[i], if_recv.at[i], over)

    for i in range(CHUNKS):
        chunk(i).start()

    def columns(shard):
        return pl.ds(pl.multiple_of(shard * depth, LANES), depth)

    mine = pl.ds(pl.multiple_of(core * tokens, 128), tokens)
    partner_cross = (1 - chip) * 2 + 1 - core
    swaps = [
        remote(lens, len_v.at[core], core_send.at[0], core_recv.at[0], beside),
        remote(outf.at[0], of_v.at[dp], core_send.at[1], core_recv.at[1], beside),
        remote(grad.at[0], grad_v.at[mine, :], core_send.at[2], core_recv.at[2], beside),
        remote(act.at[0, :, columns(partner)], act_v.at[0, mine, :], core_send.at[3], core_recv.at[3], beside),
        remote(act.at[0, :, columns(partner_cross)], act_v.at[1, mine, :], core_send.at[4], core_recv.at[4], beside),
    ]
    for copy in swaps:
        copy.start()
    local = [
        pltpu.make_async_copy(act.at[0, :, columns(dp)], act_v.at[0, mine, :], local_sem.at[0]),
        pltpu.make_async_copy(act.at[0, :, columns(cross)], act_v.at[1, mine, :], local_sem.at[1]),
        pltpu.make_async_copy(grad.at[0], grad_v.at[mine, :], local_sem.at[2]),
        pltpu.make_async_copy(inf.at[0], if_v.at[0], local_sem.at[3]),
        pltpu.make_async_copy(outf.at[0], of_v.at[dp], local_sem.at[4]),
        pltpu.make_async_copy(lens, len_v.at[core], local_sem.at[5]),
    ]
    for copy in local:
        copy.start()
    for r in range(ROUNDS):
        for peer in near:
            pl.semaphore_signal(rounds.at[r], inc=1, device_id=peer, device_id_type=MESH)
        pl.semaphore_wait(rounds.at[r], len(near))
    pl.semaphore_signal(rounds.at[ROUNDS], inc=1, device_id=beside, device_id_type=MESH)
    pl.semaphore_wait(rounds.at[ROUNDS], 1)

    relay = remote(of_v.at[cross], of_v.at[cross], core_send.at[5], core_recv.at[5], beside)

    for copy in local:
        copy.wait()
    for copy in swaps:
        copy.wait()

    def contract(block):
        def body(i, carry):
            rows = pl.ds(pl.multiple_of(i * step, LANES), step)
            if block == 1:
                chunk(i).wait_recv()
            product = jnp.dot(act_v[block, :, rows], if_v[block, rows, :], preferred_element_type=jnp.float32)
            if block == 0:
                pi[...] = jnp.where(i == 0, product, pi[...] + product)
            else:
                pi[...] += product
            return carry

        lax.fori_loop(0, CHUNKS, body, 0)

    out_over.wait()
    relay.start()
    pi[...] = jnp.zeros_like(pi)
    contract(0)
    relay.wait()

    seqs = tokens // SLOT
    row = lax.broadcasted_iota(jnp.int32, (2 * tokens, 1), 0)
    limit = jnp.zeros((2 * tokens, 1), jnp.int32)
    for s in range(2 * seqs):
        count = len_v[s // seqs][:, s % seqs : s % seqs + 1]
        limit = jnp.where(row // SLOT == s, count, limit)
    live = (row % SLOT < limit).astype(jnp.float32)
    total = jnp.zeros(po.shape, jnp.float32)
    for shard in range(4):
        total += jnp.dot(
            grad_v[:, shard * odepth : (shard + 1) * odepth], of_v[shard], preferred_element_type=jnp.float32
        )
    po[...] = total * live
    contract(1)

    width = QUERIES * RANK
    lanes = lax.broadcasted_iota(jnp.int32, (width, LANES), 1)
    fold = (lax.broadcasted_iota(jnp.int32, (width, LANES), 0) // RANK == lanes % QUERIES).astype(jnp.bfloat16)
    score = jnp.sum((po[...] * pi[...]).reshape(2 * seqs, SLOT, width), axis=1)
    high = score.astype(jnp.bfloat16).astype(jnp.float32)
    middle = (score - high).astype(jnp.bfloat16).astype(jnp.float32)
    parts = jnp.concatenate([high, middle, score - high - middle], axis=0).astype(jnp.bfloat16)
    score = jnp.sum(
        jnp.dot(parts, fold, preferred_element_type=jnp.float32).reshape(3, 2 * seqs, LANES), axis=0
    )
    spot = lax.broadcasted_iota(jnp.int32, (2 * seqs, LANES), 1) // QUERIES
    keep = spot == lax.broadcasted_iota(jnp.int32, (2 * seqs, LANES), 0)
    value = jnp.sum(jnp.where(keep, score, 0.0), axis=0, keepdims=True)

    waiting = [chunk(i) for i in range(CHUNKS)]

    def exchange(value, rx, me, sends):
        rx[me] = value
        copies = [remote(rx.at[me], rx.at[me], s, r, device) for s, r, device in sends]
        for copy in copies:
            copy.start()
        for copy in copies:
            copy.wait_recv()
        waiting.extend(copies)
        result = rx[0]
        for j in range(1, rx.shape[0]):
            result = result + rx[j]
        return result

    value = exchange(
        value, rx1, core * nx + x, [(send1.at[i], recv1.at[i], peer1(d, o)) for i, (d, o) in enumerate(first)]
    )
    value = exchange(
        value, rx2, y * nz + z, [(send2.at[i], recv2.at[i], peer2(d, e)) for i, (d, e) in enumerate(second)]
    )

    own = lax.broadcasted_iota(jnp.int32, (8, LANES), 0) + core * seqs
    lane = lax.broadcasted_iota(jnp.int32, (8, LANES), 1)
    spread = jnp.where(lane // QUERIES == own, jnp.broadcast_to(value, (8, LANES)), 0.0)
    for shift in (8, 16, 32, 64):
        spread += pltpu.roll(spread, shift, 1)
    out[...] = spread[:seqs, :QUERIES] * jnp.float32(1 / math.sqrt(RANK * SLOT * blocks))
    for copy in waiting:
        copy.wait_send()


def shards(activations, gradients, input_factor, output_factor, lengths):
    blocks = lax.axis_size("layer")
    dims = LAYER_DIMS[blocks]
    ny, nz, nx = dims
    tokens = activations.shape[1]
    depth, width = input_factor.shape[1:]
    odepth = output_factor.shape[1]
    seqs = lengths.shape[0]
    bf16, f32 = jnp.bfloat16, jnp.float32
    dma = pltpu.SemaphoreType.DMA
    anywhere = pl.BlockSpec(memory_space=pl.ANY)
    inputs = (activations, gradients, input_factor, output_factor, lengths.reshape(1, seqs))
    return pl.pallas_call(
        functools.partial(kernel, dims, blocks),
        out_shape=jax.ShapeDtypeStruct((seqs, QUERIES), f32),
        in_specs=[anywhere] * 5,
        out_specs=pl.BlockSpec(memory_space=pltpu.VMEM),
        scratch_shapes=[
            pltpu.VMEM((2, 2 * tokens, depth), bf16),
            pltpu.VMEM((2 * tokens, 4 * odepth), bf16),
            pltpu.VMEM((4, odepth, width), bf16),
            pltpu.VMEM((2, depth, width), bf16),
            pltpu.VMEM((2, 1, seqs), jnp.int32),
            pltpu.VMEM((2 * tokens, width), f32),
            pltpu.VMEM((2 * tokens, width), f32),
            pltpu.VMEM((2 * nx, 1, LANES), f32),
            pltpu.VMEM((ny * nz, 1, LANES), f32),
            dma((6,)),
            dma, dma,
            dma((6,)), dma((6,)),
            dma((CHUNKS,)), dma((CHUNKS,)),
            pltpu.SemaphoreType.REGULAR((ROUNDS + 1,)),
            dma((2 * nx,)), dma((2 * nx,)),
            dma((ny * nz,)), dma((ny * nz,)),
        ],
        compiler_params=pltpu.CompilerParams(collective_id=0, has_side_effects=True, vmem_limit_bytes=32 << 20),
    )(*[pltpu.with_memory_space_constraint(a, pltpu.HBM) for a in inputs])


def solution(mesh):
    in_specs = (
        P("layer", "dp", None),
        P("layer", "dp", None),
        P("layer", "dp", None),
        P("layer", "dp", None),
        P("dp"),
    )
    out_specs = P("dp", None)
    return jax.shard_map(shards, mesh=mesh, in_specs=in_specs, out_specs=out_specs, check_vma=False)
```

```python
import functools
import math

import jax
import jax.numpy as jnp
from jax import lax
from jax.experimental import pallas as pl
from jax.experimental.pallas import tpu as pltpu
from jax.sharding import PartitionSpec as P

RANK = 32
QUERIES = 8
SLOT = 32
LANES = 128
MESH = pl.DeviceIdType.MESH
LAYER_DIMS = {256: (8, 4, 8), 8: (2, 2, 2), 4: (2, 1, 2)}
CHUNKS = 8
ROUNDS = 7


def kernel(
    dims, blocks, act, grad, inf, outf, lens, out,
    act_v, grad_v, of_v, if_v, len_v, pi, po, rx1, rx2,
    local_sem, out_send, out_recv, core_send, core_recv, if_send, if_recv,
    rounds, send1, recv1, send2, recv2,
):
    ny, nz, nx = dims
    layer, dp = lax.axis_index("layer"), lax.axis_index("dp")
    x = lax.rem(layer, nx)
    z = lax.rem(layer // nx, nz)
    y = layer // (nx * nz)
    core = lax.rem(dp, 2)
    chip = dp // 2
    partner = chip * 2 + 1 - core
    cross = (1 - chip) * 2 + core
    tokens, depth = act.shape[1], inf.shape[1]
    odepth = outf.shape[1]
    step = depth // CHUNKS

    def at(y_, z_, x_):
        return (y_ * nz + z_) * nx + x_

    def far_first(n):
        return sorted(range(1, n), key=lambda d: -min(d, n - d))

    first = [(d, o) for d in far_first(nx) for o in (0, 1)] + [(0, 1)]

    def peer1(d, o):
        c = core if o == 0 else 1 - core
        return {"layer": at(y, z, lax.rem(x + d, nx)), "dp": chip * 2 + c}

    second = [(d, e) for d in range(ny) for e in range(nz) if d or e]
    second.sort(key=lambda t: -min(t[0], ny - t[0]) - 2 * min(t[1], nz - t[1]))

    def peer2(d, e):
        return {"layer": at(lax.rem(y + d, ny), lax.rem(z + e, nz), x), "dp": dp}

    def remote(src, dst, send, recv, device):
        return pltpu.make_async_remote_copy(
            src_ref=src, dst_ref=dst, send_sem=send, recv_sem=recv, device_id=device, device_id_type=MESH
        )

    over = {"layer": layer, "dp": cross}
    beside = {"layer": layer, "dp": partner}

    barrier = pltpu.get_barrier_semaphore()
    next_z = {"layer": at(y, lax.rem(z + 2 * chip + nz - 1, nz), x), "dp": cross}
    near = [over, next_z, peer1(1, 0), peer1(nx - 1, 0), peer2(1, 0), peer2(ny - 1, 0)]
    for peer in [*near, beside]:
        pl.semaphore_signal(barrier, inc=1, device_id=peer, device_id_type=MESH)
    pl.semaphore_wait(barrier, len(near) + 1)

    out_over = remote(outf.at[0], of_v.at[dp], out_send, out_recv, over)
    out_over.start()

    def chunk(i):
        rows = pl.ds(pl.multiple_of(i * step, 16), step)
        return remote(inf.at[0, rows, :], if_v.at[1, rows, :], if_send.at[i], if_recv.at[i], over)

    for i in range(CHUNKS):
        chunk(i).start()

    def columns(shard):
        return pl.ds(pl.multiple_of(shard * depth, LANES), depth)

    mine = pl.ds(pl.multiple_of(core * tokens, 128), tokens)
    partner_cross = (1 - chip) * 2 + 1 - core
    swaps = [
        remote(lens, len_v.at[core], core_send.at[0], core_recv.at[0], beside),
        remote(outf.at[0], of_v.at[dp], core_send.at[1], core_recv.at[1], beside),
        remote(grad.at[0], grad_v.at[mine, :], core_send.at[2], core_recv.at[2], beside),
        remote(act.at[0, :, columns(partner)], act_v.at[0, mine, :], core_send.at[3], core_recv.at[3], beside),
        remote(act.at[0, :, columns(partner_cross)], act_v.at[1, mine, :], core_send.at[4], core_recv.at[4], beside),
    ]
    for copy in swaps:
        copy.start()
    local = [
        pltpu.make_async_copy(act.at[0, :, columns(dp)], act_v.at[0, mine, :], local_sem.at[0]),
        pltpu.make_async_copy(act.at[0, :, columns(cross)], act_v.at[1, mine, :], local_sem.at[1]),
        pltpu.make_async_copy(grad.at[0], grad_v.at[mine, :], local_sem.at[2]),
        pltpu.make_async_copy(inf.at[0], if_v.at[0], local_sem.at[3]),
        pltpu.make_async_copy(outf.at[0], of_v.at[dp], local_sem.at[4]),
        pltpu.make_async_copy(lens, len_v.at[core], local_sem.at[5]),
    ]
    for copy in local:
        copy.start()
    for r in range(ROUNDS):
        for peer in near:
            pl.semaphore_signal(rounds.at[r], inc=1, device_id=peer, device_id_type=MESH)
        pl.semaphore_wait(rounds.at[r], len(near))
    pl.semaphore_signal(rounds.at[ROUNDS], inc=1, device_id=beside, device_id_type=MESH)
    pl.semaphore_wait(rounds.at[ROUNDS], 1)

    relay = remote(of_v.at[cross], of_v.at[cross], core_send.at[5], core_recv.at[5], beside)

    for copy in local:
        copy.wait()
    for copy in swaps:
        copy.wait()

    def contract(block):
        def body(i, carry):
            rows = pl.ds(pl.multiple_of(i * step, LANES), step)
            if block == 1:
                chunk(i).wait_recv()
            product = jnp.dot(act_v[block, :, rows], if_v[block, rows, :], preferred_element_type=jnp.float32)
            if block == 0:
                pi[...] = jnp.where(i == 0, product, pi[...] + product)
            else:
                pi[...] += product
            return carry

        lax.fori_loop(0, CHUNKS - block, body, 0)

    out_over.wait()
    relay.start()
    pi[...] = jnp.zeros_like(pi)
    contract(0)
    relay.wait()

    seqs = tokens // SLOT
    row = lax.broadcasted_iota(jnp.int32, (2 * tokens, 1), 0)
    limit = jnp.zeros((2 * tokens, 1), jnp.int32)
    for s in range(2 * seqs):
        count = len_v[s // seqs][:, s % seqs : s % seqs + 1]
        limit = jnp.where(row // SLOT == s, count, limit)
    live = (row % SLOT < limit).astype(jnp.float32)
    total = jnp.zeros(po.shape, jnp.float32)
    for shard in range(4):
        total += jnp.dot(
            grad_v[:, shard * odepth : (shard + 1) * odepth], of_v[shard], preferred_element_type=jnp.float32
        )
    po[...] = total * live
    contract(1)

    width = QUERIES * RANK
    lanes = lax.broadcasted_iota(jnp.int32, (width, LANES), 1)
    fold = (lax.broadcasted_iota(jnp.int32, (width, LANES), 0) // RANK == lanes % QUERIES).astype(jnp.bfloat16)
    tail = pl.ds((CHUNKS - 1) * step, step)
    chunk(CHUNKS - 1).wait_recv()
    last = jnp.dot(act_v[1, :, tail], if_v[1, tail, :], preferred_element_type=jnp.float32)
    score = jnp.sum((po[...] * (pi[...] + last)).reshape(2 * seqs, SLOT, width), axis=1)
    high = score.astype(jnp.bfloat16).astype(jnp.float32)
    middle = (score - high).astype(jnp.bfloat16).astype(jnp.float32)
    parts = jnp.concatenate([high, middle, score - high - middle], axis=0).astype(jnp.bfloat16)
    score = jnp.sum(
        jnp.dot(parts, fold, preferred_element_type=jnp.float32).reshape(3, 2 * seqs, LANES), axis=0
    )
    spot = lax.broadcasted_iota(jnp.int32, (2 * seqs, LANES), 1) // QUERIES
    keep = spot == lax.broadcasted_iota(jnp.int32, (2 * seqs, LANES), 0)
    value = jnp.sum(jnp.where(keep, score, 0.0), axis=0, keepdims=True)

    waiting = [chunk(i) for i in range(CHUNKS)]

    def exchange(value, rx, me, sends):
        rx[me] = value
        copies = [remote(rx.at[me], rx.at[me], s, r, device) for s, r, device in sends]
        for copy in copies:
            copy.start()
        for copy in copies:
            copy.wait_recv()
        waiting.extend(copies)
        terms = [rx[j] for j in range(rx.shape[0])]
        while len(terms) > 1:
            terms = [a + b for a, b in zip(terms[::2], terms[1::2])]
        return terms[0]

    value = exchange(
        value, rx1, core * nx + x, [(send1.at[i], recv1.at[i], peer1(d, o)) for i, (d, o) in enumerate(first)]
    )
    value = exchange(
        value, rx2, y * nz + z, [(send2.at[i], recv2.at[i], peer2(d, e)) for i, (d, e) in enumerate(second)]
    )

    own = lax.broadcasted_iota(jnp.int32, (8, LANES), 0) + core * seqs
    lane = lax.broadcasted_iota(jnp.int32, (8, LANES), 1)
    spread = jnp.where(lane // QUERIES == own, jnp.broadcast_to(value, (8, LANES)), 0.0)
    for shift in (8, 16, 32, 64):
        spread += pltpu.roll(spread, shift, 1)
    out[...] = spread[:seqs, :QUERIES] * jnp.float32(1 / math.sqrt(RANK * SLOT * blocks))
    for copy in waiting:
        copy.wait_send()


def shards(activations, gradients, input_factor, output_factor, lengths):
    blocks = lax.axis_size("layer")
    dims = LAYER_DIMS[blocks]
    ny, nz, nx = dims
    tokens = activations.shape[1]
    depth, width = input_factor.shape[1:]
    odepth = output_factor.shape[1]
    seqs = lengths.shape[0]
    bf16, f32 = jnp.bfloat16, jnp.float32
    dma = pltpu.SemaphoreType.DMA
    anywhere = pl.BlockSpec(memory_space=pl.ANY)
    inputs = (activations, gradients, input_factor, output_factor, lengths.reshape(1, seqs))
    return pl.pallas_call(
        functools.partial(kernel, dims, blocks),
        out_shape=jax.ShapeDtypeStruct((seqs, QUERIES), f32),
        in_specs=[anywhere] * 5,
        out_specs=pl.BlockSpec(memory_space=pltpu.VMEM),
        scratch_shapes=[
            pltpu.VMEM((2, 2 * tokens, depth), bf16),
            pltpu.VMEM((2 * tokens, 4 * odepth), bf16),
            pltpu.VMEM((4, odepth, width), bf16),
            pltpu.VMEM((2, depth, width), bf16),
            pltpu.VMEM((2, 1, seqs), jnp.int32),
            pltpu.VMEM((2 * tokens, width), f32),
            pltpu.VMEM((2 * tokens, width), f32),
            pltpu.VMEM((2 * nx, 1, LANES), f32),
            pltpu.VMEM((ny * nz, 1, LANES), f32),
            dma((6,)),
            dma, dma,
            dma((6,)), dma((6,)),
            dma((CHUNKS,)), dma((CHUNKS,)),
            pltpu.SemaphoreType.REGULAR((ROUNDS + 1,)),
            dma((2 * nx,)), dma((2 * nx,)),
            dma((ny * nz,)), dma((ny * nz,)),
        ],
        compiler_params=pltpu.CompilerParams(collective_id=0, has_side_effects=True, vmem_limit_bytes=32 << 20),
    )(*[pltpu.with_memory_space_constraint(a, pltpu.HBM) for a in inputs])


def solution(mesh):
    in_specs = (
        P("layer", "dp", None),
        P("layer", "dp", None),
        P("layer", "dp", None),
        P("layer", "dp", None),
        P("dp"),
    )
    out_specs = P("dp", None)
    return jax.shard_map(shards, mesh=mesh, in_specs=in_specs, out_specs=out_specs, check_vma=False)
```
